32 devices in a mesh: grp: 2 (over y), row: 4 (over z), col: 2 (over core), chan: 2 (over x).
Axes of the slice: x: 2, y: 2, z: 4, core: 2. Of those that a mesh axis runs over, the one named last changes fastest.
Arguments:
- theta: bfloat16 [2048, 16, 1024], P(('grp', 'row'), None, ('col', 'chan')), parts along dimension 0, may hold values from -6 to 6
- left_env: bfloat16 [2048, 12, 1024], P(('grp', 'row')), parts along dimension 0, may hold values from -0.25 to 0.25
- right_env: bfloat16 [2048, 12, 1024], P('grp', None, ('col', 'chan')), parts along dimension 0, may hold values from -0.078125 to 0.078125
- mpo_left: float32 [12, 12, 4, 4], replicated, may hold values from -0.875 to 0.875
- mpo_right: float32 [12, 12, 4, 4], replicated, may hold values from -0.875 to 0.875
Outputs:
- residual: bfloat16 [2048, 16384], P(('grp', 'col', 'chan'), 'row'), parts along dimension 0
- hvp: bfloat16 [2048, 16, 1024], P(('grp', 'row'), None, ('col', 'chan')), parts along dimension 0
The draws below stay inside these ranges and needn't reach their ends.
There are 2 independent parts, one for each index of `grp`. The reference program is written for one: setup_inputs(seed, part) draws one part's arguments, and reference() takes and returns one part's arrays. A program takes and returns all parts, laid end to end along the dimension named above; an argument that names none is the same for every part. Nothing has to cross between parts.
All inputs are finite; a program needn't handle non-finite values.
Results may differ from the reference program's by a relative error of at most 0.025.
Values may be sent and summed in bfloat16 or wider, within the bound.
A program may use at most 128 MiB of HBM per device.

```python
import jax
import jax.numpy as jnp
from jax import lax

D = 1024
W = 12
PHYS = 4
S = 16


def with_spikes(values, rng, source, target, shards_of, factor):
    owner, partner = [(jnp.arange(values.shape[dim]) // (values.shape[dim] // shards_of)).reshape([-1 if axis == dim else 1 for axis in range(values.ndim)]) for dim in (source, target)]
    chosen = jax.random.permutation(rng, shards_of)[partner]
    strong = (owner == chosen) | (owner == (partner + shards_of // 2) % shards_of)
    return jnp.where(strong, factor * values, values)


def block_scale(key, extent, shards, least, top_value):
    gain, own = 1.0, jax.random.fold_in(key, 6)
    for dim, parts in shards:
        draws = jnp.exp(jax.random.uniform(jax.random.fold_in(own, dim), (parts,), jnp.float32, least / len(shards), top_value / len(shards)))
        gain = gain * jnp.repeat(draws, extent[dim] // parts).reshape([-1 if axis == dim else 1 for axis in range(len(extent))])
    return gain


def normal_values(stream_key, shape, scale, most, cuts=(), kind=jnp.bfloat16):
    entries = jax.random.normal(stream_key, shape, jnp.float32) * scale
    if len(cuts) > 0:
        entries = block_scale(stream_key, shape, cuts, -0.22, 0.18) * entries
    return jnp.clip(entries, min=-most, max=most).astype(kind)


def gaussian_with(own_key, extent, spread, bound, shards, heavy, held_as=jnp.bfloat16):
    result = spread * jax.random.normal(own_key, extent, jnp.float32)
    if shards:
        result = result * block_scale(own_key, extent, shards, -0.22, 0.18)
    return jnp.clip(with_spikes(result, jax.random.fold_in(own_key, 3), *heavy), -bound, bound).astype(held_as)


def setup_inputs(seed: int = 0, part: int = 0) -> dict:
    arg_keys = jax.random.split(jax.random.key(seed), 6)
    part_keys = jax.random.split(jax.random.fold_in(arg_keys[5], part), 6)
    return {
        "theta": normal_values(part_keys[0], (D, S, D), 1.0, 6.0, ((0, 4), (2, 4))),
        "left_env": gaussian_with(part_keys[1], (D, W, D), D ** -0.5, 0.25, ((0, 4),), (0, 2, 4, 2.0)),
        "right_env": gaussian_with(part_keys[2], (D, W, D), (W * D) ** -0.5, 0.078125, ((2, 4),), (2, 0, 4, 2.0)),
        "mpo_left": normal_values(arg_keys[3], (W, W, PHYS, PHYS), (W * PHYS) ** -0.5, 0.875, (), jnp.float32),
        "mpo_right": normal_values(arg_keys[4], (W, W, PHYS, PHYS), (W * PHYS) ** -0.5, 0.875, (), jnp.float32),
    }


def mpo_product(mpo_left, mpo_right):
    paired = jnp.einsum('wuxs,uvyt->wstxyv', mpo_left, mpo_right, precision=lax.Precision.HIGHEST)
    return paired.reshape(W * PHYS * PHYS, PHYS * PHYS * W).astype(jnp.bfloat16)


def rounded(values):
    return lax.optimization_barrier(values.astype(jnp.bfloat16)).astype(jnp.float32)


def reference(theta, left_env, right_env, mpo_left, mpo_right):
    mpo_pair = mpo_product(mpo_left, mpo_right).astype(jnp.float32)
    theta_wide = theta.astype(jnp.float32)
    right_wide = right_env.astype(jnp.float32)
    stride = min(64, D)
    blocks = D // stride

    def step(total, index):
        begin = (index * stride).astype(jnp.int32)
        left_block = lax.dynamic_slice_in_dim(left_env, begin, stride, 0).astype(jnp.float32)
        section_one = rounded(jnp.einsum('awk,ksb->awsb', left_block, theta_wide))
        section_three = rounded(jnp.einsum('pq,apb->aqb', mpo_pair, section_one.reshape(stride, W * S, D)))
        section_three = section_three.reshape(stride, S, W, D)
        partial_res = jnp.einsum('kvb,asvb->kas', right_wide, section_three).reshape(D, stride * S)
        resid_block = partial_res.astype(jnp.bfloat16)
        back_one = rounded(jnp.einsum('kp,kvb->pvb', rounded(partial_res), right_wide))
        back_one = back_one.reshape(stride, S * W, D)
        back_two = rounded(jnp.einsum('pq,aqb->apb', mpo_pair, back_one)).reshape(stride, W, S, D)
        total = total + jnp.einsum('awk,awsb->ksb', left_block, back_two)
        return total, resid_block

    total, resid_blocks = lax.scan(step, jnp.zeros((D, S, D), jnp.float32), jnp.arange(blocks, dtype=jnp.int32))
    residual = jnp.transpose(resid_blocks, (1, 0, 2)).reshape(D, D * S)
    return residual, total.astype(jnp.bfloat16)
```

```python
import functools

import jax
import jax.numpy as jnp
from jax import lax
from jax.experimental import pallas as pl
from jax.experimental.pallas import tpu as pltpu
from jax.sharding import PartitionSpec as P

PAD = 16
LIMIT = 52 * 1024 * 1024


def cost(flops, size):
    return pl.CostEstimate(flops=int(flops), bytes_accessed=int(size), transcendentals=0)


def params():
    return pltpu.CompilerParams(dimension_semantics=("arbitrary",), vmem_limit_bytes=LIMIT)


def dot(lhs, rhs):
    return jnp.dot(lhs, rhs, preferred_element_type=jnp.float32)


def forward_kernel(theta_ref, left_ref, mpo_ref, out_ref, lhs, held):
    blocks, rows, width = theta_ref.shape
    channels = left_ref.shape[0]
    tile, _, pairs, lanes = held.shape
    for r in range(blocks):
        lhs[:, r * width : (r + 1) * width] = theta_ref[r]

    def one(w, carry):
        part = dot(lhs[...], left_ref[w]).astype(jnp.bfloat16)
        held[:, w] = part.reshape(tile, pairs, lanes)
        return carry

    lax.fori_loop(0, channels, one, 0, unroll=2)

    def two(b, carry):
        part = dot(mpo_ref[...], held[b].reshape(channels * pairs, lanes)).astype(jnp.bfloat16)
        out_ref[:, b] = part.reshape(out_ref.shape[0], PAD, lanes)
        return carry

    lax.fori_loop(0, tile, two, 0, unroll=8)


def forward(theta, left, mpo, pairs, tile):
    blocks, rows, width = theta.shape
    channels, depth, lanes = left.shape
    bonds = rows // pairs
    step = tile * pairs
    flops = 2 * rows * depth * channels * lanes + 2 * bonds * mpo.size * lanes
    return pl.pallas_call(
        forward_kernel,
        grid=(bonds // tile,),
        out_shape=jax.ShapeDtypeStruct((pairs, bonds, PAD, lanes), jnp.bfloat16),
        in_specs=[
            pl.BlockSpec((blocks, step, width), lambda i: (0, i, 0)),
            pl.BlockSpec(left.shape, lambda i: (0, 0, 0), pipeline_mode=pl.Buffered(1)),
            pl.BlockSpec(mpo.shape, lambda i: (0, 0), pipeline_mode=pl.Buffered(1)),
        ],
        out_specs=pl.BlockSpec((pairs, tile, PAD, lanes), lambda i: (0, i, 0, 0)),
        scratch_shapes=[
            pltpu.VMEM((step, depth), jnp.bfloat16),
            pltpu.VMEM((tile, channels, pairs, lanes), jnp.bfloat16),
        ],
        compiler_params=params(),
        cost_estimate=cost(flops, 2 * (theta.size + left.size + pairs * bonds * PAD * lanes)),
    )(theta, left, mpo)


def residual_kernel(has_total, right_ref, three_ref, *refs):
    out_ref = refs[-1]
    parts, _, rows, lanes = out_ref.shape
    depth = right_ref.shape[1]
    part = dot(right_ref[...], three_ref[0].reshape(depth, lanes))
    part = part.reshape(parts, rows, lanes)
    if has_total:
        part = part + refs[0][:, 0]
    out_ref[:, 0] = part.astype(out_ref.dtype)


def residual_term(right, three, total, chunk, first, count, parts, dtype):
    pairs, bonds, _, lanes = three.shape
    rows = right.shape[0]
    depth = bonds * PAD
    block = (parts, 1, rows // parts, lanes)
    operands = [right, three]
    specs = [
        pl.BlockSpec((rows, depth), lambda i: (0, chunk), pipeline_mode=pl.Buffered(1)),
        pl.BlockSpec((1, bonds, PAD, lanes), lambda i: (first + i, 0, 0, 0)),
    ]
    if total is not None:
        operands.append(total)
        specs.append(pl.BlockSpec(block, lambda i: (0, first + i, 0, 0)))
    aliases = {2: 0} if total is not None and dtype == jnp.float32 else {}
    return pl.pallas_call(
        functools.partial(residual_kernel, total is not None),
        grid=(count,),
        out_shape=jax.ShapeDtypeStruct((parts, count, rows // parts, lanes), dtype),
        in_specs=specs,
        out_specs=pl.BlockSpec(block, lambda i: (0, i, 0, 0)),
        input_output_aliases=aliases,
        compiler_params=params(),
        cost_estimate=cost(2 * rows * depth * count * lanes, count * lanes * (2 * depth + 8 * rows)),
    )(*operands)


def backward_kernel(groups, right_ref, *refs):
    res_refs = refs[:groups]
    mpo_ref, left_ref, out_ref, held, lhs = refs[groups:]
    tile, _, _, lanes = held.shape
    channels = lhs.shape[1] // lanes
    pairs = lhs.shape[0] // tile
    width = out_ref.shape[2]
    begin = 0
    for res_ref in res_refs:
        parts, count, rows, _ = res_ref.shape

        def five(x, carry, res_ref=res_ref, begin=begin, depth=parts * rows):
            part = dot(right_ref[...], res_ref[:, x].reshape(depth, lanes)).astype(jnp.bfloat16)
            held[:, begin + x] = part.reshape(tile, PAD, lanes)
            return carry

        lax.fori_loop(0, count, five, 0, unroll=2)
        begin += count

    def six(b, carry):
        part = dot(mpo_ref[...], held[b].reshape(begin * PAD, lanes)).astype(jnp.bfloat16)
        where = pl.ds(pl.multiple_of(b * pairs, pairs), pairs)
        for w in range(channels):
            lhs[where, w * lanes : (w + 1) * lanes] = part[w * pairs : (w + 1) * pairs]
        return carry

    lax.fori_loop(0, tile, six, 0, unroll=8)

    for r in range(out_ref.shape[0]):
        out_ref[r] = dot(lhs[...], left_ref[:, r * width : (r + 1) * width]).astype(jnp.bfloat16)


def backward(right, residuals, mpo, left, chunk, bonds, pairs, blocks, tile):
    depth, lanes = residuals[0].shape[0] * residuals[0].shape[2], residuals[0].shape[3]
    channels = left.shape[0] // lanes
    width = left.shape[1] // blocks
    steps = bonds // tile
    counts = sum(res.shape[1] for res in residuals)
    flops = 2 * bonds * (PAD * depth * counts * lanes + mpo.size * lanes + pairs * left.size)
    size = 2 * (depth * counts * lanes + left.size + bonds * PAD * depth + bonds * pairs * left.shape[1])
    whole = [
        pl.BlockSpec(res.shape, lambda i: (0, 0, 0, 0), pipeline_mode=pl.Buffered(1))
        for res in residuals
    ]
    return pl.pallas_call(
        functools.partial(backward_kernel, len(residuals)),
        grid=(steps,),
        out_shape=jax.ShapeDtypeStruct((blocks, bonds * pairs, width), jnp.bfloat16),
        in_specs=[pl.BlockSpec((tile * PAD, depth), lambda i: (chunk * steps + i, 0))]
        + whole
        + [
            pl.BlockSpec(mpo.shape, lambda i: (0, 0), pipeline_mode=pl.Buffered(1)),
            pl.BlockSpec(left.shape, lambda i: (0, 0), pipeline_mode=pl.Buffered(1)),
        ],
        out_specs=pl.BlockSpec((blocks, tile * pairs, width), lambda i: (0, i, 0)),
        scratch_shapes=[
            pltpu.VMEM((tile, counts, PAD, lanes), jnp.bfloat16),
            pltpu.VMEM((tile * pairs, channels * lanes), jnp.bfloat16),
        ],
        compiler_params=params(),
        cost_estimate=cost(flops, size),
    )(right, *residuals, mpo, left)


def mpo_product(mpo_left, mpo_right):
    paired = jnp.einsum("wuxs,uvyt->wstxyv", mpo_left, mpo_right, precision=lax.Precision.HIGHEST)
    channels, phys = mpo_left.shape[0], mpo_left.shape[2]
    return paired.reshape(channels * phys * phys, phys * phys * channels).astype(jnp.bfloat16)


def tiled_shards(theta, left_env, right_env, mpo_left, mpo_right):
    lanes, channels, depth = left_env.shape
    pairs, bonds = theta.shape[1:]
    width = theta.shape[0]
    blocks = lax.axis_size("row")
    cols, chans = lax.axis_size("col"), lax.axis_size("chan")
    parts = cols * chans
    chunks = 4
    size = bonds // chunks
    tile = min(32, size)
    halves = 2
    count = pairs // halves
    rows = right_env.shape[0]

    turned = jnp.transpose(theta, (2, 1, 0)).reshape(chunks, size * pairs, width)
    gathered = [lax.all_gather(turned[c], "row", axis=0) for c in range(chunks)]

    mpo = mpo_product(mpo_left, mpo_right).reshape(channels * pairs, pairs, channels)
    mpo = jnp.pad(mpo, ((0, 0), (0, 0), (0, PAD - channels)))
    mpo_back = mpo.reshape(channels * pairs, pairs * PAD)
    mpo_front = mpo_back.T
    left_front = jnp.transpose(left_env, (1, 2, 0))
    left_back = jnp.transpose(left_env, (1, 0, 2)).reshape(channels * lanes, depth)
    right_back = jnp.transpose(right_env, (2, 1, 0))
    right_back = jnp.pad(right_back, ((0, 0), (0, PAD - channels), (0, 0)))
    right_back = right_back.reshape(bonds * PAD, rows)
    right_front = right_back.T

    total = None
    for c in range(chunks - 1):
        three = forward(gathered[c], left_front, mpo_front, pairs, tile)
        total = residual_term(right_front, three, total, c, 0, pairs, parts, jnp.float32)
    three = forward(gathered[-1], left_front, mpo_front, pairs, tile)
    kept, residuals = [], []
    for h in range(halves):
        term = residual_term(
            right_front, three, total, chunks - 1, h * count, count, parts, jnp.bfloat16
        )
        term = term.reshape(cols, chans, count, rows // parts, lanes)
        term = lax.psum_scatter(term, "col", scatter_dimension=0)
        term = lax.psum_scatter(term, "chan", scatter_dimension=0)
        kept.append(term)
    for h in range(halves):
        full = lax.all_gather(lax.all_gather(kept[h], "chan", axis=0), "col", axis=0)
        residuals.append(full.reshape(parts, count, rows // parts, lanes))

    products = []
    for c in range(chunks):
        part = backward(
            right_back, residuals, mpo_back, left_back, c, size, pairs, blocks, tile
        )
        products.append(lax.psum_scatter(part, "row", scatter_dimension=0))
    product = jnp.concatenate(products, axis=0).reshape(bonds, pairs, width)
    residual = jnp.transpose(jnp.concatenate(kept, axis=0), (1, 2, 0))
    return residual.reshape(rows // parts, lanes * pairs), jnp.transpose(product, (2, 1, 0))


def plain_shards(theta, left_env, right_env, mpo_left, mpo_right):
    left_rows, channels = left_env.shape[:2]
    pairs, right_rows = theta.shape[1:]
    mpo_pair = mpo_product(mpo_left, mpo_right)
    einsum = functools.partial(jnp.einsum, preferred_element_type=jnp.float32)
    one = einsum("awk,ksb->awsb", left_env, lax.all_gather(theta, "row", axis=0, tiled=True))
    one = one.astype(jnp.bfloat16).reshape(left_rows, channels * pairs, right_rows)
    three = einsum("pq,apb->aqb", mpo_pair, one).astype(jnp.bfloat16)
    three = three.reshape(left_rows, pairs, channels, right_rows)
    term = einsum("kvb,asvb->kas", right_env, three).astype(jnp.bfloat16)
    term = term.reshape(right_env.shape[0], left_rows * pairs)
    residual = lax.psum_scatter(term, ("col", "chan"), scatter_dimension=0, tiled=True)
    full = lax.all_gather(residual, ("col", "chan"), axis=0, tiled=True)
    back = einsum("kp,kvb->pvb", full, right_env).astype(jnp.bfloat16)
    back = back.reshape(left_rows, pairs * channels, right_rows)
    back = einsum("pq,aqb->apb", mpo_pair, back).astype(jnp.bfloat16)
    back = back.reshape(left_rows, channels, pairs, right_rows)
    product = einsum("awk,awsb->ksb", left_env, back).astype(jnp.bfloat16)
    return residual, lax.psum_scatter(product, "row", scatter_dimension=0, tiled=True)


def shards(theta, left_env, right_env, mpo_left, mpo_right):
    wide = left_env.shape[0] % 128 == 0 and theta.shape[0] % 128 == 0
    wide = wide and theta.shape[2] % 128 == 0 and theta.shape[1] == PAD
    body = tiled_shards if wide and left_env.shape[1] <= PAD else plain_shards
    return body(theta, left_env, right_env, mpo_left, mpo_right)


def solution(mesh):
    in_specs = (
        P(("grp", "row"), None, ("col", "chan")),
        P(("grp", "row"), None, None),
        P("grp", None, ("col", "chan")),
        P(),
        P(),
    )
    out_specs = (P(("grp", "col", "chan"), "row"), P(("grp", "row"), None, ("col", "chan")))
    return jax.shard_map(shards, mesh=mesh, in_specs=in_specs, out_specs=out_specs, check_vma=False)
```

```python
import functools

import jax
import jax.numpy as jnp
from jax import lax
from jax.experimental import pallas as pl
from jax.experimental.pallas import tpu as pltpu
from jax.sharding import PartitionSpec as P

PAD = 16
LIMIT = 52 * 1024 * 1024


def cost(flops, size):
    return pl.CostEstimate(flops=int(flops), bytes_accessed=int(size), transcendentals=0)


def params():
    return pltpu.CompilerParams(dimension_semantics=("arbitrary",), vmem_limit_bytes=LIMIT)


def dot(lhs, rhs):
    return jnp.dot(lhs, rhs, preferred_element_type=jnp.float32)


def pair_dot(lhs, first, second):
    return dot(lhs, jnp.concatenate([first, second], axis=1)).astype(jnp.bfloat16)


def forward_kernel(tiles, has_total, theta_ref, left_ref, mpo_ref, right_ref, *refs):
    out_ref, lhs, held, three = refs[-4:]
    blocks, _, width = theta_ref.shape
    tile, channels, pairs, lanes = held.shape
    parts, _, rows, _ = out_ref.shape
    depth = right_ref.shape[1]
    index = pl.program_id(0)

    @pl.when(index < tiles)
    def _():
        for r in range(blocks):
            lhs[:, r * width : (r + 1) * width] = theta_ref[r]

        def one(w, carry):
            part = dot(lhs[...], left_ref[w]).astype(jnp.bfloat16)
            held[:, 2 * w] = part[:, :lanes].reshape(tile, pairs, lanes)
            held[:, 2 * w + 1] = part[:, lanes:].reshape(tile, pairs, lanes)
            return carry

        lax.fori_loop(0, channels // 2, one, 0, unroll=2)

        def two(b, carry):
            first = held[2 * b].reshape(channels * pairs, lanes)
            second = held[2 * b + 1].reshape(channels * pairs, lanes)
            part = pair_dot(mpo_ref[...], first, second)
            where = index * tile + 2 * b
            three[:, where] = part[:, :lanes].reshape(three.shape[0], PAD, lanes)
            three[:, where + 1] = part[:, lanes:].reshape(three.shape[0], PAD, lanes)
            return carry

        lax.fori_loop(0, tile // 2, two, 0, unroll=4)

    @pl.when(index >= tiles)
    def _():
        x = 2 * (index - tiles)
        first, second = three[x].reshape(depth, lanes), three[x + 1].reshape(depth, lanes)
        part = dot(right_ref[...], jnp.concatenate([first, second], axis=1))
        for j in range(2):
            term = part[:, j * lanes : (j + 1) * lanes].reshape(parts, rows, lanes)
            if has_total:
                term = term + refs[0][:, j]
            out_ref[:, j] = term.astype(out_ref.dtype)


def forward(theta, left, mpo, right, total, chunk, pairs, tile, parts, dtype):
    blocks, steps, width = theta.shape
    halves, depth, twice = left.shape
    lanes, channels = twice // 2, halves * 2
    bonds = steps // pairs
    tiles = bonds // tile
    rows = right.shape[0]
    step = tile * pairs
    flops = 2 * steps * depth * channels * lanes + 2 * bonds * mpo.size * lanes
    flops += 2 * rows * bonds * PAD * pairs * lanes
    block = (parts, 2, rows // parts, lanes)
    late = lambda i: (0, jnp.maximum(i - tiles, 0), 0, 0)
    operands = [theta, left, mpo, right]
    specs = [
        pl.BlockSpec((blocks, step, width), lambda i: (0, jnp.minimum(i, tiles - 1), 0)),
        pl.BlockSpec(left.shape, lambda i: (0, 0, 0), pipeline_mode=pl.Buffered(1)),
        pl.BlockSpec(mpo.shape, lambda i: (0, 0), pipeline_mode=pl.Buffered(1)),
        pl.BlockSpec((rows, bonds * PAD), lambda i: (0, chunk), pipeline_mode=pl.Buffered(1)),
    ]
    if total is not None:
        operands.append(total)
        specs.append(pl.BlockSpec(block, late))
    aliases = {4: 0} if total is not None and dtype == jnp.float32 else {}
    size = 2 * (theta.size + left.size + rows * bonds * PAD) + 8 * rows * pairs * lanes
    return pl.pallas_call(
        functools.partial(forward_kernel, tiles, total is not None),
        grid=(tiles + pairs // 2,),
        out_shape=jax.ShapeDtypeStruct((parts, pairs, rows // parts, lanes), dtype),
        in_specs=specs,
        out_specs=pl.BlockSpec(block, late),
        scratch_shapes=[
            pltpu.VMEM((step, depth), jnp.bfloat16),
            pltpu.VMEM((tile, channels, pairs, lanes), jnp.bfloat16),
            pltpu.VMEM((pairs, bonds, PAD, lanes), jnp.bfloat16),
        ],
        input_output_aliases=aliases,
        compiler_params=params(),
        cost_estimate=cost(flops, size),
    )(*operands)


def exchange_kernel(pieces, term, full, near, mine, far, sent, got):
    col, chan = lax.axis_index("col"), lax.axis_index("chan")
    chans, count, rows, lanes = mine.shape
    group = count // pieces
    core, chip = {"col": 1 - col}, {"chan": 1 - chan}
    barrier = pltpu.get_barrier_semaphore()
    for peer in (core, chip):
        pl.semaphore_signal(barrier, inc=1, device_id=peer, device_id_type=pl.DeviceIdType.MESH)
    pl.semaphore_wait(barrier, 2)

    def copy(kind, j, source, target, peer):
        return pltpu.make_async_remote_copy(
            src_ref=source,
            dst_ref=target,
            send_sem=sent.at[kind, j],
            recv_sem=got.at[kind, j],
            device_id=peer,
            device_id_type=pl.DeviceIdType.MESH,
        )

    spans = [pl.ds(j * group, group) for j in range(pieces)]
    firsts = [
        copy(0, j, term.at[1 - col, :, spans[j]], near.at[:, spans[j]], core) for j in range(pieces)
    ]
    seconds = [copy(1, j, mine.at[:, spans[j]], far.at[:, spans[j]], chip) for j in range(pieces)]
    block = pl.ds(col * chans, chans)
    thirds = [
        copy(2, j, full.at[block, spans[j]], full.at[block, spans[j]], core) for j in range(pieces)
    ]
    for item in firsts:
        item.start()
    for j in range(pieces):
        firsts[j].wait_recv()

        def first(x, carry):
            for q in range(chans):
                value = term[col, q, x].astype(jnp.float32) + near[q, x].astype(jnp.float32)
                mine[q, x] = value.astype(jnp.bfloat16)
            return carry

        lax.fori_loop(j * group, (j + 1) * group, first, 0)
        seconds[j].start()
    for j in range(pieces):
        seconds[j].wait_recv()

        def second(x, carry):
            for q in range(chans):
                value = mine[q, x].astype(jnp.float32) + far[q, x].astype(jnp.float32)
                full[col * chans + q, x] = value.astype(jnp.bfloat16)
            return carry

        lax.fori_loop(j * group, (j + 1) * group, second, 0)
        thirds[j].start()
    for j in range(pieces):
        thirds[j].wait_recv()
    for item in firsts + seconds + thirds:
        item.wait_send()


def exchange(term):
    cols, chans, count, rows, lanes = term.shape
    pieces = 8
    half = pltpu.VMEM((chans, count, rows, lanes), jnp.bfloat16)
    return pl.pallas_call(
        functools.partial(exchange_kernel, pieces),
        out_shape=jax.ShapeDtypeStruct((cols * chans, count, rows, lanes), jnp.bfloat16),
        in_specs=[pl.BlockSpec(memory_space=pltpu.VMEM)],
        out_specs=pl.BlockSpec(memory_space=pltpu.VMEM),
        scratch_shapes=[half, half, half]
        + [pltpu.SemaphoreType.DMA((3, pieces)), pltpu.SemaphoreType.DMA((3, pieces))],
        compiler_params=pltpu.CompilerParams(
            collective_id=0, has_side_effects=True, vmem_limit_bytes=LIMIT
        ),
        cost_estimate=cost(0, 4 * term.size),
    )(term)


def backward_kernel(groups, right_ref, *refs):
    res_refs = refs[:groups]
    mpo_ref, left_ref, out_ref, held, lhs = refs[groups:]
    tile, _, _, lanes = held.shape
    channels = lhs.shape[1] // lanes
    pairs = lhs.shape[0] // tile
    width = out_ref.shape[2]
    begin = 0
    for res_ref in res_refs:
        parts, count, rows, _ = res_ref.shape

        def five(x, carry, res_ref=res_ref, begin=begin, depth=parts * rows):
            first = res_ref[:, 2 * x].reshape(depth, lanes)
            second = res_ref[:, 2 * x + 1].reshape(depth, lanes)
            part = pair_dot(right_ref[...], first, second)
            held[:, begin + 2 * x] = part[:, :lanes].reshape(tile, PAD, lanes)
            held[:, begin + 2 * x + 1] = part[:, lanes:].reshape(tile, PAD, lanes)
            return carry

        lax.fori_loop(0, count // 2, five, 0, unroll=2)
        begin += count

    def six(b, carry):
        first = held[2 * b].reshape(begin * PAD, lanes)
        second = held[2 * b + 1].reshape(begin * PAD, lanes)
        part = pair_dot(mpo_ref[...], first, second)
        for j in range(2):
            where = pl.ds(pl.multiple_of((2 * b + j) * pairs, pairs), pairs)
            half = part[:, j * lanes : (j + 1) * lanes]
            for w in range(channels):
                lhs[where, w * lanes : (w + 1) * lanes] = half[w * pairs : (w + 1) * pairs]
        return carry

    lax.fori_loop(0, tile // 2, six, 0, unroll=4)

    for r in range(0, out_ref.shape[0], 2):
        part = dot(lhs[...], left_ref[:, r * width : (r + 2) * width]).astype(jnp.bfloat16)
        out_ref[r] = part[:, :width]
        out_ref[r + 1] = part[:, width:]


def backward(right, residuals, mpo, left, chunk, bonds, pairs, blocks, tile):
    depth, lanes = residuals[0].shape[0] * residuals[0].shape[2], residuals[0].shape[3]
    channels = left.shape[0] // lanes
    width = left.shape[1] // blocks
    steps = bonds // tile
    counts = sum(res.shape[1] for res in residuals)
    flops = 2 * bonds * (PAD * depth * counts * lanes + mpo.size * lanes + pairs * left.size)
    size = 2 * (depth * counts * lanes + left.size + bonds * PAD * depth + bonds * pairs * left.shape[1])
    whole = [
        pl.BlockSpec(res.shape, lambda i: (0, 0, 0, 0), pipeline_mode=pl.Buffered(1))
        for res in residuals
    ]
    return pl.pallas_call(
        functools.partial(backward_kernel, len(residuals)),
        grid=(steps,),
        out_shape=jax.ShapeDtypeStruct((blocks, bonds * pairs, width), jnp.bfloat16),
        in_specs=[pl.BlockSpec((tile * PAD, depth), lambda i: (chunk * steps + i, 0))]
        + whole
        + [
            pl.BlockSpec(mpo.shape, lambda i: (0, 0), pipeline_mode=pl.Buffered(1)),
            pl.BlockSpec(left.shape, lambda i: (0, 0), pipeline_mode=pl.Buffered(1)),
        ],
        out_specs=pl.BlockSpec((blocks, tile * pairs, width), lambda i: (0, i, 0)),
        scratch_shapes=[
            pltpu.VMEM((tile, counts, PAD, lanes), jnp.bfloat16),
            pltpu.VMEM((tile * pairs, channels * lanes), jnp.bfloat16),
        ],
        compiler_params=params(),
        cost_estimate=cost(flops, size),
    )(right, *residuals, mpo, left)


def mpo_product(mpo_left, mpo_right):
    paired = jnp.einsum("wuxs,uvyt->wstxyv", mpo_left, mpo_right, precision=lax.Precision.HIGHEST)
    channels, phys = mpo_left.shape[0], mpo_left.shape[2]
    return paired.reshape(channels * phys * phys, phys * phys * channels).astype(jnp.bfloat16)


def tiled_shards(theta, left_env, right_env, mpo_left, mpo_right):
    lanes, channels, depth = left_env.shape
    pairs, bonds = theta.shape[1:]
    width = theta.shape[0]
    blocks = lax.axis_size("row")
    cols, chans = lax.axis_size("col"), lax.axis_size("chan")
    parts = cols * chans
    chunks = 4
    size = bonds // chunks
    tile = min(32, size)
    rows = right_env.shape[0]

    turned = jnp.transpose(theta, (2, 1, 0)).reshape(chunks, size * pairs, width)
    gathered = [lax.all_gather(turned[c], "row", axis=0) for c in range(chunks)]

    mpo = mpo_product(mpo_left, mpo_right).reshape(channels * pairs, pairs, channels)
    mpo = jnp.pad(mpo, ((0, 0), (0, 0), (0, PAD - channels)))
    mpo_back = mpo.reshape(channels * pairs, pairs * PAD)
    mpo_front = mpo_back.T
    left_front = left_env.reshape(lanes, channels // 2, 2, depth)
    left_front = jnp.transpose(left_front, (1, 3, 2, 0)).reshape(channels // 2, depth, 2 * lanes)
    left_back = jnp.transpose(left_env, (1, 0, 2)).reshape(channels * lanes, depth)
    right_back = jnp.transpose(right_env, (2, 1, 0))
    right_back = jnp.pad(right_back, ((0, 0), (0, PAD - channels), (0, 0)))
    right_back = right_back.reshape(bonds * PAD, rows)
    right_front = right_back.T

    total = None
    for c in range(chunks):
        dtype = jnp.bfloat16 if c == chunks - 1 else jnp.float32
        total = forward(
            gathered[c], left_front, mpo_front, right_front, total, c, pairs, tile, parts, dtype
        )
    full = exchange(total.reshape(cols, chans, pairs, rows // parts, lanes))
    mine = lax.axis_index("col") * chans + lax.axis_index("chan")
    kept = lax.dynamic_index_in_dim(full, mine, 0, keepdims=False)
    residuals = [full]

    products = []
    for c in range(chunks):
        part = backward(
            right_back, residuals, mpo_back, left_back, c, size, pairs, blocks, tile
        )
        products.append(lax.psum_scatter(part, "row", scatter_dimension=0))
    product = jnp.concatenate(products, axis=0).reshape(bonds, pairs, width)
    residual = jnp.transpose(kept, (1, 2, 0))
    return residual.reshape(rows // parts, lanes * pairs), jnp.transpose(product, (2, 1, 0))


def plain_shards(theta, left_env, right_env, mpo_left, mpo_right):
    left_rows, channels = left_env.shape[:2]
    pairs, right_rows = theta.shape[1:]
    mpo_pair = mpo_product(mpo_left, mpo_right)
    einsum = functools.partial(jnp.einsum, preferred_element_type=jnp.float32)
    one = einsum("awk,ksb->awsb", left_env, lax.all_gather(theta, "row", axis=0, tiled=True))
    one = one.astype(jnp.bfloat16).reshape(left_rows, channels * pairs, right_rows)
    three = einsum("pq,apb->aqb", mpo_pair, one).astype(jnp.bfloat16)
    three = three.reshape(left_rows, pairs, channels, right_rows)
    term = einsum("kvb,asvb->kas", right_env, three).astype(jnp.bfloat16)
    term = term.reshape(right_env.shape[0], left_rows * pairs)
    residual = lax.psum_scatter(term, ("col", "chan"), scatter_dimension=0, tiled=True)
    full = lax.all_gather(residual, ("col", "chan"), axis=0, tiled=True)
    back = einsum("kp,kvb->pvb", full, right_env).astype(jnp.bfloat16)
    back = back.reshape(left_rows, pairs * channels, right_rows)
    back = einsum("pq,aqb->apb", mpo_pair, back).astype(jnp.bfloat16)
    back = back.reshape(left_rows, channels, pairs, right_rows)
    product = einsum("awk,awsb->ksb", left_env, back).astype(jnp.bfloat16)
    return residual, lax.psum_scatter(product, "row", scatter_dimension=0, tiled=True)


def shards(theta, left_env, right_env, mpo_left, mpo_right):
    wide = left_env.shape[0] % 128 == 0 and theta.shape[0] % 128 == 0
    wide = wide and theta.shape[2] % 128 == 0 and theta.shape[1] == PAD
    wide = wide and lax.axis_size("col") == 2 and lax.axis_size("chan") == 2
    wide = wide and left_env.shape[1] % 2 == 0 and lax.axis_size("row") % 2 == 0
    body = tiled_shards if wide and left_env.shape[1] <= PAD else plain_shards
    return body(theta, left_env, right_env, mpo_left, mpo_right)


def solution(mesh):
    in_specs = (
        P(("grp", "row"), None, ("col", "chan")),
        P(("grp", "row"), None, None),
        P("grp", None, ("col", "chan")),
        P(),
        P(),
    )
    out_specs = (P(("grp", "col", "chan"), "row"), P(("grp", "row"), None, ("col", "chan")))
    return jax.shard_map(shards, mesh=mesh, in_specs=in_specs, out_specs=out_specs, check_vma=False)
```
